32 devices in a mesh: expert: 16 (over z, y, x), etp: 2 (over core).
Axes of the slice: x: 2, y: 2, z: 4, core: 2. Of those that a mesh axis runs over, the one named last changes fastest.
Arguments:
- grad_out: bfloat16 [2048, 3584], P('expert', 'etp'), may hold values from -6 to 6
- combine: bfloat16 [2048, 8], P('expert'), may hold values from 0.099609375 to 2.5
- expert_ids: int32 [2048, 8], P('expert'), may hold values from 0 to 31, all different within a row; in each aligned block of 128 rows (0 to 127, 128 to 255, ...) at most 64 rows name the same one
- saved_gate: bfloat16 [1024, 32, 1024], P(None, 'expert', 'etp'), may hold values from -6 to 6
- saved_up: bfloat16 [1024, 32, 1024], P(None, 'expert', 'etp'), may hold values from -1.5 to 1.5
- gate_weight: bfloat16 [32, 3584, 1024], P('expert', None, 'etp'), may hold values from -0.09375 to 0.09375
- up_weight: bfloat16 [32, 3584, 1024], P('expert', None, 'etp'), may hold values from -0.09375 to 0.09375
- down_weight: bfloat16 [32, 1024, 3584], P('expert', 'etp'), may hold values from -0.09375 to 0.09375
Outputs:
- grad_tokens: bfloat16 [2048, 3584], P('expert', 'etp')
- grad_combine: bfloat16 [2048, 8], P('expert')
The draws below stay inside these ranges and needn't reach their ends.
Inputs may be any that keep to these rules, and one draw needn't show every extreme that they name: `expert_ids`: each token names 8 different experts. Among the 128 tokens of one block (one index of expert), at most 64 name any one expert, and some blocks reach that bound.
All inputs are finite; a program needn't handle non-finite values.
Results may differ from the reference program's by a relative error of at most 0.012.
Values may be sent and summed in bfloat16 or wider, within the bound.
A program may use at most 192 MiB of HBM per device.

```python
import math
import jax
import jax.numpy as jnp
import numpy as np
from jax import lax

D = 3584
FF = 1024
TOP = 8
TOK_DEV = 128
EXPERTS = 32
TOKENS = 2048
CAP = 64
SLOT_ROWS = 1024
N_EXPERT = 16
N_ETP = 2


def steps_of(stream_key, extent, shards, smallest, top_value):
    gain = 1.0
    for axis_at, parts in shards:
        draws = jax.random.uniform(jax.random.fold_in(jax.random.fold_in(stream_key, 6), axis_at), (parts,), jnp.float32, smallest / len(shards), top_value / len(shards))
        gain = gain * jnp.repeat(jnp.exp(draws), extent[axis_at] // parts).reshape((-1,) + (1,) * (len(extent) - 1 - axis_at))
    return gain


def shared_out(rng, own, number, rows, amount, top, limit, slope):
    sequence = jax.random.permutation(rng, amount)
    crowded, ordinary = portions_of(amount, rows * top, limit, slope, True), portions_of(amount, rows * top, limit, slope, False)
    places = jnp.arange(amount)

    def named(sizes, rotation):
        used = int((sizes > 0).sum())
        fixed = max(1, used // 4)
        passed = fixed + (places - fixed + rotation * (used - fixed)) % max(1, amount - fixed)
        return jnp.zeros((amount,), jnp.int32).at[sequence[jnp.where(places < fixed, places, passed)]].set(jnp.asarray(sizes, jnp.int32))

    sizes = jnp.where(number % 4 == 0, named(crowded, number // 4), named(ordinary, number - number // 4 - 1))
    mixed = jax.random.permutation(jax.random.fold_in(own, 3), amount)
    source_of, taker = mixed[0:amount // 2 * 2:2], mixed[1:amount // 2 * 2:2]
    room = jnp.minimum(sizes[source_of] - 1, limit - sizes[taker]) // 2
    room = jnp.where((source_of == sequence[0]) | (taker == sequence[0]) | (sizes[taker] == 0), 0, jnp.maximum(room, 0))
    passed = jax.random.randint(jax.random.fold_in(own, 4), (amount // 2,), 0, 1 << 20) % (room + 1)
    sizes = sizes.at[source_of].add(-passed).at[taker].add(passed)
    labels = jnp.searchsorted(jnp.cumsum(sizes), jnp.arange(rows * top), side="right").astype(jnp.int32)
    grid = labels.reshape(top, rows).T
    grid = grid[jax.random.permutation(jax.random.fold_in(own, 1), rows)]
    rotation = jax.random.randint(jax.random.fold_in(own, 2), (rows, 1), 0, top)
    return jnp.take_along_axis(grid, (jnp.arange(top)[None, :] + rotation) % top, axis=1)


def portions_of(count, total, bound, slope, full):
    loads = [(1 << 20) // math.isqrt(standing ** slope) + 1 for standing in range(1, count + 1)]
    largest = bound if full else min(bound, max(-(-total // count), total * loads[0] // sum(loads)))
    least = 1 if total - largest >= count - 1 else 0
    given, spare = [largest] + [least] * (count - 1), total - largest - least * (count - 1)
    while spare > 0:
        free = [i for i in range(1, count) if given[i] < largest] or [i for i in range(1, count) if given[i] < bound]
        whole, remaining = sum([loads[i] for i in free]), spare
        for i in free:
            more = min(bound - given[i], max(1, remaining * loads[i] // whole), spare)
            given[i] = given[i] + more
            spare = spare - more
    return np.array(given)


def gaussian(key, extent, spread, most, cuts=(), held_as=jnp.bfloat16):
    level = steps_of(key, extent, cuts, -0.22, 0.18) if cuts else 1.0
    drawn = jax.random.normal(key, extent, jnp.float32) * spread * level
    return jnp.minimum(jnp.maximum(drawn, -most), most).astype(held_as)


def setup_inputs(seed: int = 0) -> dict:
    keys = jax.random.split(jax.random.key(seed), 9)
    grad_out = gaussian(keys[0], (TOKENS, D), 1.0, 6.0, ((0, 16), (1, 2)))
    combine = jnp.clip(jnp.exp(math.log(2.5) - 3.2227897 * jax.random.uniform(keys[1], (TOKENS, TOP), jnp.float32) ** steps_of(keys[1], (TOKENS, TOP), ((0, 16),), -0.2, 0.2)), 0.099609375, 2.5).astype(jnp.bfloat16)
    expert_ids_keys = jax.random.split(jax.random.fold_in(keys[2], 1), TOKENS // TOK_DEV)
    expert_ids_turns = jax.random.permutation(jax.random.fold_in(keys[2], 3), TOKENS // TOK_DEV)
    expert_ids = jax.vmap(lambda own, number: shared_out(jax.random.fold_in(keys[2], 2), own, number, TOK_DEV, EXPERTS, TOP, CAP, 2))(expert_ids_keys, expert_ids_turns).reshape((TOKENS, TOP))
    saved_gate = gaussian(keys[3], (SLOT_ROWS, EXPERTS, FF), 1.0, 6.0, ((1, 16), (2, 2)))
    saved_up = gaussian(keys[4], (SLOT_ROWS, EXPERTS, FF), 0.1, 1.5, ((1, 16), (2, 2)))
    gate_weight = gaussian(keys[5], (EXPERTS, D, FF), D ** -0.5, 0.09375, ((0, 16), (2, 2)))
    up_weight = gaussian(keys[6], (EXPERTS, D, FF), D ** -0.5, 0.09375, ((0, 16), (2, 2)))
    down_weight = gaussian(keys[7], (EXPERTS, FF, D), D ** -0.5, 0.09375, ((0, 16), (1, 2)))
    return dict(grad_out=grad_out, combine=combine, expert_ids=expert_ids, saved_gate=saved_gate, saved_up=saved_up, gate_weight=gate_weight, up_weight=up_weight, down_weight=down_weight)


def reference(grad_out, combine, expert_ids, saved_gate, saved_up, gate_weight, up_weight, down_weight):
    token_total, top_count = expert_ids.shape
    experts, model_width, hidden = gate_weight.shape
    groups = N_EXPERT
    token_count = token_total // groups
    capacity = saved_gate.shape[0] // groups
    slot_total = groups * capacity
    grouped = expert_ids.reshape(groups, token_count, top_count)
    matches = grouped[..., None] == jnp.arange(experts, dtype=jnp.int32)
    expert_loads = jnp.sum(matches.astype(jnp.int32), axis=2)
    earlier = jnp.cumsum(expert_loads, axis=1) - expert_loads
    position = jnp.sum(jnp.where(matches, earlier[:, :, None, :], 0), axis=3)
    row_index = (jnp.arange(groups, dtype=jnp.int32)[:, None, None] * capacity + position).reshape(token_total, top_count)
    slot_owner = jnp.full((slot_total, experts), token_total * top_count, jnp.int32)
    slot_owner = slot_owner.at[row_index.reshape(-1), expert_ids.reshape(-1)].set(
        jnp.arange(token_total * top_count, dtype=jnp.int32))
    grad_padded = jnp.concatenate([grad_out, jnp.zeros((1, model_width), jnp.bfloat16)], axis=0)
    weight_padded = jnp.concatenate([combine.reshape(-1).astype(jnp.float32), jnp.zeros((1,), jnp.float32)])
    half_hidden = hidden // N_ETP

    def per_expert(running, expert):
        grad_acc, weight_acc = running
        slot_ids = lax.dynamic_index_in_dim(slot_owner, expert, 1, keepdims=False)
        token_of = slot_ids // top_count
        slot_rows = jnp.take(grad_padded, token_of, axis=0)
        slot_weight = jnp.take(weight_padded, slot_ids, axis=0)
        gate_value = lax.dynamic_index_in_dim(saved_gate, expert, 1, keepdims=False).astype(jnp.float32)
        up_value = lax.dynamic_index_in_dim(saved_up, expert, 1, keepdims=False).astype(jnp.float32)
        down_expert = lax.dynamic_index_in_dim(down_weight, expert, 0, keepdims=False)
        gate_expert = lax.dynamic_index_in_dim(gate_weight, expert, 0, keepdims=False)
        up_expert = lax.dynamic_index_in_dim(up_weight, expert, 0, keepdims=False)
        grad_hidden = jnp.dot(slot_rows, down_expert.T, preferred_element_type=jnp.float32)
        gate_sigmoid = jax.nn.sigmoid(gate_value)
        activated = gate_value * gate_sigmoid
        product = grad_hidden * activated * up_value
        weight_halves = jnp.sum(product.reshape(slot_total, N_ETP, half_hidden), axis=2).astype(jnp.bfloat16)
        weight_halves = lax.optimization_barrier(weight_halves).astype(jnp.float32)
        slot_dw = jnp.sum(weight_halves, axis=1).astype(jnp.bfloat16)
        scaled = slot_weight[:, None] * grad_hidden
        grad_gate = (scaled * up_value * gate_sigmoid * (1.0 + gate_value * (1.0 - gate_sigmoid))).astype(jnp.bfloat16)
        grad_up = (scaled * activated).astype(jnp.bfloat16)
        running_sum = jnp.zeros((slot_total, model_width), jnp.float32)
        for half_index in range(N_ETP):
            lower = half_index * half_hidden
            term_half = jnp.dot(grad_gate[:, lower:lower + half_hidden], gate_expert[:, lower:lower + half_hidden].T,
                                preferred_element_type=jnp.float32)
            term_half = term_half + jnp.dot(grad_up[:, lower:lower + half_hidden], up_expert[:, lower:lower + half_hidden].T,
                                            preferred_element_type=jnp.float32)
            term_half = lax.optimization_barrier(term_half.astype(jnp.bfloat16))
            running_sum = running_sum + term_half.astype(jnp.float32)
        slot_grad = running_sum.astype(jnp.bfloat16)
        grad_acc = grad_acc.at[token_of].add(slot_grad.astype(jnp.float32), mode="drop")
        weight_acc = weight_acc.at[slot_ids].set(slot_dw.astype(jnp.float32), mode="drop")
        return (grad_acc, weight_acc), None

    start = (jnp.zeros((token_total, model_width), jnp.float32), jnp.zeros((token_total * top_count,), jnp.float32))
    final, _ = lax.scan(per_expert, start, jnp.arange(experts, dtype=jnp.int32))
    grad_tokens = final[0].astype(jnp.bfloat16)
    grad_combine = final[1].reshape(token_total, top_count).astype(jnp.bfloat16)
    return grad_tokens, grad_combine
```

```python
import jax
import jax.numpy as jnp
from jax import lax
from jax.sharding import PartitionSpec as P


def on_device(
    grad_out, combine, expert_ids, saved_gate, saved_up, gate_weight, up_weight, down_weight
):
    groups = lax.axis_size("expert")
    per_group = gate_weight.shape[0]
    tokens = grad_out.shape[0]
    capacity = saved_gate.shape[0] // groups
    hidden = saved_gate.shape[2]
    experts = groups * per_group
    chosen = expert_ids[:, :, None] == jnp.arange(experts, dtype=jnp.int32)[None, None, :]
    weights = jnp.sum(jnp.where(chosen, combine[:, :, None].astype(jnp.float32), 0.0), axis=1)
    weights = weights.astype(jnp.bfloat16).reshape(tokens, groups, per_group)
    weights = lax.all_to_all(
        weights.transpose(1, 2, 0), "expert", split_axis=0, concat_axis=0, tiled=True
    )
    rows = lax.all_gather(grad_out, "expert", axis=0, tiled=True)
    rows = lax.all_gather(rows, "etp", axis=1, tiled=True)
    rows = rows.reshape(groups, tokens, -1)
    named = (weights > 0).astype(jnp.float32)
    position = jnp.cumsum(named, axis=2) - named
    slot = jnp.where(named > 0, position, -1.0)
    select = slot[:, :, None, :] == jnp.arange(capacity, dtype=jnp.float32)[None, None, :, None]
    scale = jnp.sum(jnp.where(select, weights[:, :, None, :].astype(jnp.float32), 0.0), axis=3)
    scale = scale.transpose(1, 0, 2)[..., None]
    select = select.astype(jnp.bfloat16)
    slot_rows = jnp.einsum(
        "blct,btd->lbcd", select, rows, preferred_element_type=jnp.bfloat16
    )
    grad_hidden = jnp.einsum(
        "lbcd,lfd->lbcf", slot_rows, down_weight, preferred_element_type=jnp.float32
    )
    gate_value = saved_gate.reshape(groups, capacity, per_group, hidden).transpose(2, 0, 1, 3)
    up_value = saved_up.reshape(groups, capacity, per_group, hidden).transpose(2, 0, 1, 3)
    gate_value = gate_value.astype(jnp.float32)
    up_value = up_value.astype(jnp.float32)
    gate_sigmoid = jax.nn.sigmoid(gate_value)
    activated = gate_value * gate_sigmoid
    weight_part = jnp.sum(grad_hidden * activated * up_value, axis=3)
    scaled = scale * grad_hidden
    grad_gate = (
        scaled * up_value * gate_sigmoid * (1.0 + gate_value * (1.0 - gate_sigmoid))
    ).astype(jnp.bfloat16)
    grad_up = (scaled * activated).astype(jnp.bfloat16)
    weight_tok = jnp.einsum(
        "blct,lbc->blt", select, weight_part.astype(jnp.bfloat16),
        preferred_element_type=jnp.float32,
    ).astype(jnp.bfloat16)
    weight_tok = lax.psum(weight_tok, "etp")
    weight_tok = lax.all_to_all(weight_tok, "expert", split_axis=0, concat_axis=0, tiled=True)
    weight_tok = weight_tok.transpose(2, 0, 1).reshape(tokens, 1, experts)
    grad_combine = jnp.sum(
        jnp.where(chosen, weight_tok.astype(jnp.float32), 0.0), axis=2
    ).astype(jnp.bfloat16)
    partial = jnp.einsum(
        "lbcf,ldf->lbcd", grad_gate, gate_weight, preferred_element_type=jnp.float32
    )
    partial = partial + jnp.einsum(
        "lbcf,ldf->lbcd", grad_up, up_weight, preferred_element_type=jnp.float32
    )
    partial = jnp.einsum(
        "blct,lbcd->btd", select, partial.astype(jnp.bfloat16),
        preferred_element_type=jnp.float32,
    ).astype(jnp.bfloat16)
    partial = partial.reshape(groups * tokens, -1)
    partial = lax.psum_scatter(partial, "etp", scatter_dimension=1, tiled=True)
    grad_tokens = lax.psum_scatter(partial, "expert", scatter_dimension=0, tiled=True)
    return (grad_tokens, grad_combine)


def solution(mesh):
    in_specs = (
        P("expert", "etp"),
        P("expert", None),
        P("expert", None),
        P(None, "expert", "etp"),
        P(None, "expert", "etp"),
        P("expert", None, "etp"),
        P("expert", None, "etp"),
        P("expert", "etp", None),
    )
    out_specs = (P("expert", "etp"), P("expert", None))
    return jax.shard_map(
        on_device, mesh=mesh, in_specs=in_specs, out_specs=out_specs, check_vma=False
    )
```
